32 devices in a mesh: gx: 4 (over y, x), gy: 2 (over core), gz: 4 (over z).
Axes of the slice: x: 2, y: 2, z: 4, core: 2. Of those that a mesh axis runs over, the one named last changes fastest.
Arguments:
- tokens: bfloat16 [192, 12288], P(('gy', 'gz'), 'gx'), may hold values from -6 to 6
- grad_out: bfloat16 [192, 12288], P(('gy', 'gz'), 'gx'), may hold values from -0.86328125 to 0.86328125
- w_in: bfloat16 [12288, 24576], P('gx', ('gy', 'gz')), may hold values from -0.0546875 to 0.0546875
- w_out: bfloat16 [24576, 12288], P(('gy', 'gz'), 'gx'), may hold values from -0.0390625 to 0.0390625
Outputs:
- output: float32 [192, 12288], P(('gy', 'gz'), 'gx')
- grad_in: float32 [192, 12288], P(('gy', 'gz'), 'gx')
- grad_w_in: bfloat16 [12288, 24576], P('gx', ('gy', 'gz'))
- grad_w_out: bfloat16 [24576, 12288], P(('gy', 'gz'), 'gx')
The draws below stay inside these ranges and needn't reach their ends.
All inputs are finite; a program needn't handle non-finite values.
Results may differ from the reference program's by a relative error of at most 0.0049.
Values may be sent and summed in bfloat16 or wider, within the bound.
A program may use at most 128 MiB of HBM per device.

```python
import jax
import jax.numpy as jnp

D = 12288
FF = 24576
TOKENS = 192


def levels(stream_key, dims, pieces, least, top_value):
    loudness = 1.0
    for dim, shards_of in pieces:
        steps = jax.random.uniform(jax.random.fold_in(jax.random.fold_in(stream_key, 6), dim), (shards_of,), jnp.float32, least / len(pieces), top_value / len(pieces))
        loudness = loudness * jnp.repeat(jnp.exp(steps), dims[dim] // shards_of).reshape((-1,) + (1,) * (len(dims) - 1 - dim))
    return loudness


def gaussian(own_key, shape, spread, reach, split=(), held_as=jnp.bfloat16):
    entries = spread * jax.random.normal(own_key, shape, jnp.float32)
    if split:
        entries = entries * levels(own_key, shape, split, -0.22, 0.18)
    return jnp.clip(entries, -reach, reach).astype(held_as)


def setup_inputs(seed: int = 0) -> dict:
    arg_keys = jax.random.split(jax.random.key(seed), 5)
    tokens = gaussian(arg_keys[0], (TOKENS, D), 1.0, 6.0, ((0, 8), (1, 4)))
    grad_out = gaussian(arg_keys[1], (TOKENS, D), (2.0 / TOKENS ** 0.5), 0.86328125, ((0, 8), (1, 4)))
    w_in = gaussian(arg_keys[2], (D, FF), D ** -0.5, 0.0546875, ((0, 4), (1, 8)))
    w_out = gaussian(arg_keys[3], (FF, D), FF ** -0.5, 0.0390625, ((0, 8), (1, 4)))
    return dict(tokens=tokens, grad_out=grad_out, w_in=w_in, w_out=w_out)


def gelu_parts(pre_sum):
    scale_c = 0.7978845608
    inner_arg = scale_c * (pre_sum + 0.044715 * pre_sum * pre_sum * pre_sum)
    tanh_val = jnp.tanh(inner_arg)
    value = 0.5 * pre_sum * (1.0 + tanh_val)
    deriv = 0.5 * (1.0 + tanh_val) + 0.5 * pre_sum * (1.0 - tanh_val * tanh_val) * scale_c * (1.0 + 3.0 * 0.044715 * pre_sum * pre_sum)
    return value, deriv


def reference(tokens, grad_out, w_in, w_out):
    pre_sum = jnp.dot(tokens, w_in, preferred_element_type=jnp.float32)
    back_sum = jnp.dot(grad_out, w_out.T, preferred_element_type=jnp.float32)
    value, deriv = gelu_parts(pre_sum)
    hidden = value.astype(jnp.bfloat16)
    slopes = (back_sum * deriv).astype(jnp.bfloat16)
    output = jnp.dot(hidden, w_out, preferred_element_type=jnp.float32)
    grad_in = jnp.dot(slopes, w_in.T, preferred_element_type=jnp.float32)
    grad_w_in = jnp.dot(tokens.T, slopes, preferred_element_type=jnp.float32).astype(jnp.bfloat16)
    grad_w_out = jnp.dot(hidden.T, grad_out, preferred_element_type=jnp.float32).astype(jnp.bfloat16)
    return output, grad_in, grad_w_in, grad_w_out
```

```python
import functools
import math

import jax
import jax.numpy as jnp
from jax import lax
from jax.experimental import pallas as pl
from jax.experimental.pallas import tpu as pltpu
from jax.sharding import PartitionSpec as P

MESH = pl.DeviceIdType.MESH
NN = (((1,), (0,)), ((), ()))
NT = (((1,), (1,)), ((), ()))
TN_DIMS = (((0,), (0,)), ((), ()))


def gelu_parts(pre):
    scale_c = 0.7978845608
    t = jnp.tanh(scale_c * (pre + 0.044715 * pre * pre * pre))
    value = 0.5 * pre * (1.0 + t)
    deriv = 0.5 * (1.0 + t) + 0.5 * pre * (1.0 - t * t) * scale_c * (
        1.0 + 3.0 * 0.044715 * pre * pre
    )
    return value, deriv


def weight_grads_kernel(tok, slo, hid, grd, o_in, o_out):
    o_in[...] = lax.dot_general(
        tok[...], slo[...], TN_DIMS, preferred_element_type=jnp.float32
    ).astype(jnp.bfloat16)
    o_out[...] = lax.dot_general(
        hid[...], grd[...], TN_DIMS, preferred_element_type=jnp.float32
    ).astype(jnp.bfloat16)


def weight_grads(tok, slo, hid, grd):
    rows, width = tok.shape
    units = slo.shape[1]
    steps = math.gcd(math.gcd(width // 128, units // 128), 12)
    tw, tu = width // steps, units // steps
    return pl.pallas_call(
        weight_grads_kernel,
        grid=(steps,),
        in_specs=[
            pl.BlockSpec((rows, tw), lambda i: (0, i)),
            pl.BlockSpec((rows, units), lambda i: (0, 0)),
            pl.BlockSpec((rows, tu), lambda i: (0, i)),
            pl.BlockSpec((rows, width), lambda i: (0, 0)),
        ],
        out_specs=[
            pl.BlockSpec((tw, units), lambda i: (i, 0)),
            pl.BlockSpec((tu, width), lambda i: (i, 0)),
        ],
        out_shape=[
            jax.ShapeDtypeStruct((width, units), jnp.bfloat16),
            jax.ShapeDtypeStruct((units, width), jnp.bfloat16),
        ],
        compiler_params=pltpu.CompilerParams(vmem_limit_bytes=48 * 1024 * 1024),
        cost_estimate=pl.CostEstimate(
            flops=4 * rows * width * units,
            bytes_accessed=4 * width * units,
            transcendentals=0,
        ),
    )(tok, slo, hid, grd)


def fused_kernel(
    sizes, tok_ref, grd_ref, win_hbm, wout_hbm,
    out_ref, gin_ref, tok_all, grd_all, hid_all, slo_all,
    win, wout, lhs, acc, part, rbuf, own, act, deriv,
    obuf, ohalf, yrecv, zf, zsend, zrecv,
    wsem, lsem, zss, zrs, yss, yrs, rss, rrs, ass, ars, css, crs, dss, drs,
):
    X, Y, Z = sizes["gx"], sizes["gy"], sizes["gz"]
    gx, gy, gz = lax.axis_index("gx"), lax.axis_index("gy"), lax.axis_index("gz")
    R, D = tok_ref.shape
    T, F = hid_all.shape
    C, H = T // X, Z * R
    TN = math.gcd(math.gcd(F, D), 768)
    NF, ND = F // TN, D // TN
    f32, bf16 = jnp.float32, jnp.bfloat16

    def to(axis, me, k):
        return {axis: lax.rem(me + k, sizes[axis])}

    def rem(src, dst, ss, rs, axis, me, k):
        return pltpu.make_async_remote_copy(
            src_ref=src, dst_ref=dst, send_sem=ss, recv_sem=rs,
            device_id=to(axis, me, k), device_id_type=MESH,
        )

    pltpu.make_async_copy(win_hbm, win, wsem.at[0]).start()
    pltpu.make_async_copy(wout_hbm, wout, wsem.at[1]).start()

    barrier = pltpu.get_barrier_semaphore()
    for axis, me in (("gx", gx), ("gy", gy), ("gz", gz)):
        for k in range(1, sizes[axis]):
            pl.semaphore_signal(barrier, inc=1, device_id=to(axis, me, k), device_id_type=MESH)
    pl.semaphore_wait(barrier, X + Y + Z - 3)

    srcs, alls = (tok_ref, grd_ref), (tok_all, grd_all)

    def block(ref, y, z):
        return ref.at[pl.ds(pl.multiple_of((y * Z + z) * R, 8), R)]

    def zcopy(a, k):
        return rem(srcs[a], block(alls[a], gy, gz), zss.at[a, k - 1], zrs.at[a, k - 1], "gz", gz, k)

    def zarrive(a, k):
        b = block(alls[a], gy, lax.rem(gz - k + Z, Z))
        return rem(b, b, zss.at[a, k - 1], zrs.at[a, k - 1], "gz", gz, k)

    def ycopy(a, p, j):
        b = block(alls[a], gy, lax.rem(gz - j + Z, Z))
        return rem(srcs[a] if j == 0 else b, b, yss.at[a, p - 1, j], yrs.at[a, p - 1, j], "gy", gy, p)

    def yarrive(a, p, j):
        b = block(alls[a], lax.rem(gy - p + Y, Y), lax.rem(gz - j + Z, Z))
        return rem(b, b, yss.at[a, p - 1, j], yrs.at[a, p - 1, j], "gy", gy, p)

    def mine(a):
        return pltpu.make_async_copy(srcs[a], block(alls[a], gy, gz), lsem.at[a])

    def gather_start(a):
        for k in range(Z - 1, 0, -1):
            zcopy(a, k).start()
        for p in range(1, Y):
            ycopy(a, p, 0).start()
        mine(a).start()

    def gather_forward(a):
        for j in range(1, Z):
            zarrive(a, j).wait_recv()
            for p in range(1, Y):
                ycopy(a, p, j).start()

    def gather_finish(a):
        mine(a).wait()
        for p in range(1, Y):
            for j in range(Z):
                yarrive(a, p, j).wait_recv()
        load = pltpu.make_async_copy(alls[a], lhs.at[a], lsem.at[2 + a])
        load.start()
        load.wait()

    def cols(t):
        return pl.ds(pl.multiple_of(t * TN, TN), TN)

    def chunk(i):
        return pl.ds(pl.multiple_of(i * C, 16), C)

    def half(i):
        return pl.ds(pl.multiple_of(i * H, 16), H)

    def rcopy(a, t, k):
        return rem(
            part.at[a, chunk(lax.rem(gx + k, X)), cols(t)], rbuf.at[a, k - 1, :, cols(t)],
            rss.at[a, t, k - 1], rrs.at[a, t, k - 1], "gx", gx, k,
        )

    def acopy(a, t, k):
        b = act.at[a, chunk(gx), cols(t)]
        return rem(b, b, ass.at[a, t, k - 1], ars.at[a, t, k - 1], "gx", gx, k)

    def aarrive(a, t, k):
        b = act.at[a, chunk(lax.rem(gx - k + X, X)), cols(t)]
        return rem(b, b, ass.at[a, t, k - 1], ars.at[a, t, k - 1], "gx", gx, k)

    def ccopy(a, n, p):
        return rem(
            obuf.at[a, half(lax.rem(gy + p, Y)), cols(n)], yrecv.at[a, p - 1, :, cols(n)],
            css.at[a, n, p - 1], crs.at[a, n, p - 1], "gy", gy, p,
        )

    def dcopy(a, n, k):
        return rem(
            zsend.at[a, lax.rem(gz + k, Z), :, cols(n)], zrecv.at[a, k - 1, :, cols(n)],
            dss.at[a, n, k - 1], drs.at[a, n, k - 1], "gz", gz, k,
        )

    def loop(n, body):
        lax.fori_loop(0, n, lambda i, c: (body(i), c)[1], 0)

    def up(a, w, transposed):
        def body(t):
            if transposed:
                acc[...] = lax.dot_general(lhs[a], w[cols(t), :], NT, preferred_element_type=f32)
            else:
                acc[...] = lax.dot_general(lhs[a], w[:, cols(t)], NN, preferred_element_type=f32)
            part[a, :, cols(t)] = acc[...].astype(bf16)
            own[a, :, cols(t)] = acc[chunk(gx), :]
            for k in range(1, X):
                rcopy(a, t, k).start()
        loop(NF, body)

    def summed(a, t):
        for k in range(1, X):
            rcopy(a, t, k).wait_recv()
        total = own[a, :, cols(t)]
        for k in range(1, X):
            total = total + rbuf[a, k - 1, :, cols(t)].astype(f32)
        return total

    def publish(a, t, value):
        act[a, chunk(gx), cols(t)] = value.astype(bf16)
        for k in range(1, X):
            acopy(a, t, k).start()

    gather_start(0)
    gather_forward(0)
    gather_start(1)
    gather_finish(0)
    pltpu.make_async_copy(win_hbm, win, wsem.at[0]).wait()
    up(0, win, False)
    gather_forward(1)
    gather_finish(1)
    pltpu.make_async_copy(wout_hbm, wout, wsem.at[1]).wait()
    up(1, wout, True)

    def hidden_step(t):
        value, slope = gelu_parts(summed(0, t))
        deriv[:, cols(t)] = slope
        publish(0, t, value)

    loop(NF, hidden_step)
    loop(NF, lambda t: publish(1, t, summed(1, t) * deriv[:, cols(t)]))

    keeps = (hid_all, slo_all)

    def scatter_step(a, n):
        for p in range(1, Y):
            ccopy(a, n, p).wait_recv()
        total = ohalf[a, :, cols(n)]
        for p in range(1, Y):
            total = total + yrecv[a, p - 1, :, cols(n)].astype(f32)
        for z in range(Z):
            rows = total[z * R : (z + 1) * R]
            zf[a, z, :, cols(n)] = rows
            zsend[a, z, :, cols(n)] = rows.astype(bf16)
        for k in range(1, Z):
            dcopy(a, n, k).start()

    def down(a, w, transposed):
        def arrive(t):
            for k in range(1, X):
                aarrive(a, t, k).wait_recv()
        loop(NF, arrive)
        pltpu.make_async_copy(act.at[a], keeps[a], lsem.at[4 + a]).start()

        def body(n):
            if transposed:
                acc[...] = lax.dot_general(act[a], w[cols(n), :], NT, preferred_element_type=f32)
            else:
                acc[...] = lax.dot_general(act[a], w[:, cols(n)], NN, preferred_element_type=f32)
            obuf[a, :, cols(n)] = acc[...].astype(bf16)
            ohalf[a, :, cols(n)] = acc[half(gy), :]
            for p in range(1, Y):
                ccopy(a, n, p).start()

            @pl.when(n >= 1)
            def _():
                scatter_step(a, n - 1)
        loop(ND, body)
        scatter_step(a, ND - 1)

    down(0, wout, False)
    down(1, win, True)

    for a, ref in ((0, out_ref), (1, gin_ref)):
        def last(n, a=a, ref=ref):
            for k in range(1, Z):
                dcopy(a, n, k).wait_recv()
            total = zf[a, gz, :, cols(n)]
            for k in range(1, Z):
                total = total + zrecv[a, k - 1, :, cols(n)].astype(f32)
            ref[:, cols(n)] = total
        loop(ND, last)

    for a in range(2):
        pltpu.make_async_copy(act.at[a], keeps[a], lsem.at[4 + a]).wait()
        for k in range(1, Z):
            zcopy(a, k).wait_send()
        for p in range(1, Y):
            for j in range(Z):
                ycopy(a, p, j).wait_send()

        def drain_f(t, a=a):
            for k in range(1, X):
                rcopy(a, t, k).wait_send()
                acopy(a, t, k).wait_send()
        loop(NF, drain_f)

        def drain_d(n, a=a):
            for p in range(1, Y):
                ccopy(a, n, p).wait_send()
            for k in range(1, Z):
                dcopy(a, n, k).wait_send()
        loop(ND, drain_d)


def shards(sizes, tokens, grad_out, w_in, w_out):
    X, Y, Z = sizes["gx"], sizes["gy"], sizes["gz"]
    R, D = tokens.shape
    F = w_in.shape[1]
    T = R * Y * Z
    C, H = T // X, Z * R
    TN = math.gcd(math.gcd(F, D), 768)
    NF, ND = F // TN, D // TN
    f32, bf16 = jnp.float32, jnp.bfloat16
    dma = pltpu.SemaphoreType.DMA
    any_spec = pl.BlockSpec(memory_space=pl.ANY)
    vmem_spec = pl.BlockSpec(memory_space=pltpu.VMEM)
    out, gin, tok, grd, hid, slo = pl.pallas_call(
        functools.partial(fused_kernel, sizes),
        in_specs=[any_spec] * 4,
        out_specs=[vmem_spec] * 2 + [any_spec] * 4,
        out_shape=[
            jax.ShapeDtypeStruct((R, D), f32),
            jax.ShapeDtypeStruct((R, D), f32),
            jax.ShapeDtypeStruct((T, D), bf16),
            jax.ShapeDtypeStruct((T, D), bf16),
            jax.ShapeDtypeStruct((T, F), bf16),
            jax.ShapeDtypeStruct((T, F), bf16),
        ],
        scratch_shapes=[
            pltpu.VMEM((D, F), bf16),
            pltpu.VMEM((F, D), bf16),
            pltpu.VMEM((2, T, D), bf16),
            pltpu.VMEM((T, TN), f32),
            pltpu.VMEM((2, T, F), bf16),
            pltpu.VMEM((2, X - 1, C, F), bf16),
            pltpu.VMEM((2, C, F), f32),
            pltpu.VMEM((2, T, F), bf16),
            pltpu.VMEM((C, F), f32),
            pltpu.VMEM((2, T, D), bf16),
            pltpu.VMEM((2, H, D), f32),
            pltpu.VMEM((2, Y - 1, H, D), bf16),
            pltpu.VMEM((2, Z, R, D), f32),
            pltpu.VMEM((2, Z, R, D), bf16),
            pltpu.VMEM((2, Z - 1, R, D), bf16),
            dma((2,)),
            dma((6,)),
            dma((2, Z - 1)),
            dma((2, Z - 1)),
            dma((2, Y - 1, Z)),
            dma((2, Y - 1, Z)),
            dma((2, NF, X - 1)),
            dma((2, NF, X - 1)),
            dma((2, NF, X - 1)),
            dma((2, NF, X - 1)),
            dma((2, ND, Y - 1)),
            dma((2, ND, Y - 1)),
            dma((2, ND, Z - 1)),
            dma((2, ND, Z - 1)),
        ],
        compiler_params=pltpu.CompilerParams(
            collective_id=0, has_side_effects=True,
            vmem_limit_bytes=63 * 1024 * 1024,
        ),
    )(tokens, grad_out, w_in, w_out)
    g_in, g_out = weight_grads(tok, slo, hid, grd)
    return out, gin, g_in, g_out


def solution(mesh):
    rows = P(("gy", "gz"), "gx")
    w_in = P("gx", ("gy", "gz"))
    return jax.shard_map(
        functools.partial(shards, dict(mesh.shape)),
        mesh=mesh,
        in_specs=(rows, rows, w_in, rows),
        out_specs=(rows, rows, w_in, rows),
        check_vma=False,
    )
```

```python
import functools
import math

import jax
import jax.numpy as jnp
from jax import lax
from jax.experimental import pallas as pl
from jax.experimental.pallas import tpu as pltpu
from jax.sharding import PartitionSpec as P

MESH = pl.DeviceIdType.MESH
NN = (((1,), (0,)), ((), ()))
NT = (((1,), (1,)), ((), ()))
TN_DIMS = (((0,), (0,)), ((), ()))


def gelu_parts(pre):
    scale_c = 0.7978845608
    t = jnp.tanh(scale_c * (pre + 0.044715 * pre * pre * pre))
    value = 0.5 * pre * (1.0 + t)
    deriv = 0.5 * (1.0 + t) + 0.5 * pre * (1.0 - t * t) * scale_c * (
        1.0 + 3.0 * 0.044715 * pre * pre
    )
    return value, deriv


def weight_grads_kernel(tok, slo, hid, grd, o_in, o_out):
    o_in[...] = lax.dot_general(
        tok[...], slo[...], TN_DIMS, preferred_element_type=jnp.float32
    ).astype(jnp.bfloat16)
    o_out[...] = lax.dot_general(
        hid[...], grd[...], TN_DIMS, preferred_element_type=jnp.float32
    ).astype(jnp.bfloat16)


def weight_grads(tok, slo, hid, grd):
    rows, width = tok.shape
    units = slo.shape[1]
    steps = math.gcd(math.gcd(width // 128, units // 128), 12)
    tw, tu = width // steps, units // steps
    return pl.pallas_call(
        weight_grads_kernel,
        grid=(steps,),
        in_specs=[
            pl.BlockSpec((rows, tw), lambda i: (0, i)),
            pl.BlockSpec((rows, units), lambda i: (0, 0)),
            pl.BlockSpec((rows, tu), lambda i: (0, i)),
            pl.BlockSpec((rows, width), lambda i: (0, 0)),
        ],
        out_specs=[
            pl.BlockSpec((tw, units), lambda i: (i, 0)),
            pl.BlockSpec((tu, width), lambda i: (i, 0)),
        ],
        out_shape=[
            jax.ShapeDtypeStruct((width, units), jnp.bfloat16),
            jax.ShapeDtypeStruct((units, width), jnp.bfloat16),
        ],
        compiler_params=pltpu.CompilerParams(vmem_limit_bytes=62 * 1024 * 1024),
        cost_estimate=pl.CostEstimate(
            flops=4 * rows * width * units,
            bytes_accessed=4 * width * units,
            transcendentals=0,
        ),
    )(tok, slo, hid, grd)


def fused_kernel(sizes, tok_ref, grd_ref, win_hbm, wout_hbm, *refs):
    gsends, refs = refs[: sizes["gz"] - 1], refs[sizes["gz"] - 1 :]
    (out_ref, gown_ref, tok_all, grd_all, hid_all, slo_all,
    win, wout, lhs, acc, part, dbuf, rbuf, own, act, deriv,
    obuf, ohalf, yrecv, zf, zsend, zrecv,
    wsem, lsem, zss, zrs, yss, yrs, rss, rrs, ass, ars, css, crs, dss, drs) = refs

    X, Y, Z = sizes["gx"], sizes["gy"], sizes["gz"]
    gx, gy, gz = lax.axis_index("gx"), lax.axis_index("gy"), lax.axis_index("gz")
    R, D = tok_ref.shape
    T, F = hid_all.shape
    C, H = T // X, Z * R
    TN = math.gcd(math.gcd(F, D), 768)
    NF, ND = F // TN, D // TN
    f32, bf16 = jnp.float32, jnp.bfloat16

    def to(axis, me, k):
        return {axis: lax.rem(me + k, sizes[axis])}

    def rem(src, dst, ss, rs, axis, me, k):
        return pltpu.make_async_remote_copy(
            src_ref=src, dst_ref=dst, send_sem=ss, recv_sem=rs,
            device_id=to(axis, me, k), device_id_type=MESH,
        )

    pltpu.make_async_copy(win_hbm, win, wsem.at[0]).start()
    pltpu.make_async_copy(wout_hbm, wout, wsem.at[1]).start()

    barrier = pltpu.get_barrier_semaphore()
    for axis, me in (("gx", gx), ("gy", gy), ("gz", gz)):
        for k in range(1, sizes[axis]):
            pl.semaphore_signal(barrier, inc=1, device_id=to(axis, me, k), device_id_type=MESH)
    pl.semaphore_wait(barrier, X + Y + Z - 3)

    srcs, alls = (tok_ref, grd_ref), (tok_all, grd_all)

    def block(ref, y, z):
        return ref.at[pl.ds(pl.multiple_of((y * Z + z) * R, 8), R)]

    def zcopy(a, k):
        return rem(srcs[a], block(alls[a], gy, gz), zss.at[a, k - 1], zrs.at[a, k - 1], "gz", gz, k)

    def zarrive(a, k):
        b = block(alls[a], gy, lax.rem(gz - k + Z, Z))
        return rem(b, b, zss.at[a, k - 1], zrs.at[a, k - 1], "gz", gz, k)

    def ycopy(a, p, j):
        b = block(alls[a], gy, lax.rem(gz - j + Z, Z))
        return rem(srcs[a] if j == 0 else b, b, yss.at[a, p - 1, j], yrs.at[a, p - 1, j], "gy", gy, p)

    def yarrive(a, p, j):
        b = block(alls[a], lax.rem(gy - p + Y, Y), lax.rem(gz - j + Z, Z))
        return rem(b, b, yss.at[a, p - 1, j], yrs.at[a, p - 1, j], "gy", gy, p)

    def mine(a):
        return pltpu.make_async_copy(srcs[a], block(alls[a], gy, gz), lsem.at[a])

    def gather_start(a):
        for k in range(Z - 1, 0, -1):
            zcopy(a, k).start()
        for p in range(1, Y):
            ycopy(a, p, 0).start()
        mine(a).start()

    def gather_forward(a):
        for j in range(1, Z):
            zarrive(a, j).wait_recv()
            for p in range(1, Y):
                ycopy(a, p, j).start()

    def gather_finish(a):
        mine(a).wait()
        for p in range(1, Y):
            for j in range(Z):
                yarrive(a, p, j).wait_recv()
        load = pltpu.make_async_copy(alls[a], lhs.at[a], lsem.at[2 + a])
        load.start()
        load.wait()

    def cols(t):
        return pl.ds(pl.multiple_of(t * TN, TN), TN)

    def chunk(i):
        return pl.ds(pl.multiple_of(i * C, 16), C)

    def half(i):
        return pl.ds(pl.multiple_of(i * H, 16), H)

    def left(t):
        return pl.ds(pl.multiple_of(t * TN, TN // 2), TN // 2)

    def right(t):
        return pl.ds(pl.multiple_of(t * TN + TN // 2, TN // 2), TN // 2)

    def hop(src, dst, sems, a, t, i, mask):
        return pltpu.make_async_remote_copy(
            src_ref=src, dst_ref=dst, send_sem=sems[0].at[a, t, i], recv_sem=sems[1].at[a, t, i],
            device_id={"gx": peer(mask)}, device_id_type=MESH,
        )

    def peer(mask):
        low = lax.rem(gx, 2)
        high = gx - low
        if mask & 1:
            low = 1 - low
        if mask & 2:
            high = 2 - high
        return high + low

    def diagonal(a, t, i):
        c = (left, right)[i](t)
        return hop(part.at[a, chunk(peer(3)), c], dbuf.at[a, :, c], (rss, rrs), a, t, i, i + 1)

    def direct(a, t, i):
        c = (left, right)[i](t)
        return hop(part.at[a, chunk(peer(i + 1)), c], rbuf.at[a, i, :, c], (rss, rrs), a, t, 2 + i, i + 1)

    def relay(a, t, i):
        c = (right, left)[i](t)
        return hop(part.at[a, chunk(peer(i + 1)), c], rbuf.at[a, i, :, c], (rss, rrs), a, t, 4 + i, i + 1)

    def relay_step(a, t):
        for i in range(2):
            diagonal(a, t, i).wait_recv()
            c = (left, right)[i](t)
            rows = chunk(peer(2 - i))
            term = part[a, rows, c].astype(f32) + dbuf[a, :, c].astype(f32)
            part[a, rows, c] = term.astype(bf16)
            relay(a, t, 1 - i).start()

    def acopy(a, t, i):
        b = act.at[a, chunk(gx), cols(t)]
        return hop(b, b, (ass, ars), a, t, i, i + 1)

    def aarrive(a, t, i):
        b = act.at[a, chunk(peer(i + 1)), cols(t)]
        return hop(b, b, (ass, ars), a, t, i, i + 1)

    def apass(a, t, i):
        b = act.at[a, chunk(peer(2 - i)), (right, left)[i](t)]
        return hop(b, b, (ass, ars), a, t, 2 + i, i + 1)

    def apassed(a, t, i):
        b = act.at[a, chunk(peer(3)), (right, left)[i](t)]
        return hop(b, b, (ass, ars), a, t, 2 + i, i + 1)

    def pass_step(a, t):
        for i in range(2):
            aarrive(a, t, i).wait_recv()
            apass(a, t, 1 - i).start()

    def ccopy(a, n, p):
        return rem(
            obuf.at[a, half(lax.rem(gy + p, Y)), cols(n)], yrecv.at[a, p - 1, :, cols(n)],
            css.at[a, n, p - 1], crs.at[a, n, p - 1], "gy", gy, p,
        )

    def dcopy(n, k):
        return rem(
            zsend.at[lax.rem(gz + k, Z), :, cols(n)], zrecv.at[k - 1, :, cols(n)],
            dss.at[n, k - 1], drs.at[n, k - 1], "gz", gz, k,
        )

    def loop(n, body):
        lax.fori_loop(0, n, lambda i, c: (body(i), c)[1], 0)

    def up(a, w, transposed):
        def body(t):
            if transposed:
                acc[...] = lax.dot_general(lhs[a], w[cols(t), :], NT, preferred_element_type=f32)
            else:
                acc[...] = lax.dot_general(lhs[a], w[:, cols(t)], NN, preferred_element_type=f32)
            part[a, :, cols(t)] = acc[...].astype(bf16)
            own[a, :, cols(t)] = acc[chunk(gx), :]
            for i in range(2):
                diagonal(a, t, i).start()
            for i in range(2):
                direct(a, t, i).start()

            @pl.when(t >= 1)
            def _():
                relay_step(a, t - 1)
        loop(NF, body)
        relay_step(a, NF - 1)

    def summed(a, t):
        for i in range(2):
            direct(a, t, i).wait_recv()
            relay(a, t, i).wait_recv()
        total = own[a, :, cols(t)]
        for i in range(2):
            total = total + rbuf[a, i, :, cols(t)].astype(f32)
        return total

    def publish(a, t, value):
        act[a, chunk(gx), cols(t)] = value.astype(bf16)
        for i in range(2):
            acopy(a, t, i).start()

    gather_start(0)
    gather_forward(0)
    gather_start(1)
    gather_finish(0)
    pltpu.make_async_copy(win_hbm, win, wsem.at[0]).wait()
    up(0, win, False)
    gather_forward(1)
    gather_finish(1)
    pltpu.make_async_copy(wout_hbm, wout, wsem.at[1]).wait()
    up(1, wout, True)

    def hidden_step(t):
        value, slope = gelu_parts(summed(0, t))
        deriv[:, cols(t)] = slope
        publish(0, t, value)

    loop(NF, hidden_step)

    def slopes_step(t):
        publish(1, t, summed(1, t) * deriv[:, cols(t)])
        pass_step(0, t)

    loop(NF, slopes_step)

    keeps = (hid_all, slo_all)

    def scatter_step(a, n):
        for p in range(1, Y):
            ccopy(a, n, p).wait_recv()
        total = ohalf[a, :, cols(n)]
        for p in range(1, Y):
            total = total + yrecv[a, p - 1, :, cols(n)].astype(f32)
        for z in range(Z):
            rows = total[z * R : (z + 1) * R]
            zf[a, z, :, cols(n)] = rows
            if a == 0:
                zsend[z, :, cols(n)] = rows.astype(bf16)
        for k in range(1, Z):
            if a == 0:
                dcopy(n, k).start()
            else:
                gsends[k - 1][:, cols(n)] = zf[a, lax.rem(gz + k, Z), :, cols(n)].astype(bf16)
        if a == 1:
            gown_ref[:, cols(n)] = zf[a, gz, :, cols(n)]

    def down(a, w, transposed):
        def arrive(t):
            for i in range(2):
                apassed(a, t, i).wait_recv()
        loop(NF, arrive)
        pltpu.make_async_copy(act.at[a], keeps[a], lsem.at[4 + a]).start()

        def body(n):
            if transposed:
                acc[...] = lax.dot_general(act[a], w[cols(n), :], NT, preferred_element_type=f32)
            else:
                acc[...] = lax.dot_general(act[a], w[:, cols(n)], NN, preferred_element_type=f32)
            obuf[a, :, cols(n)] = acc[...].astype(bf16)
            ohalf[a, :, cols(n)] = acc[half(gy), :]
            for p in range(1, Y):
                ccopy(a, n, p).start()

            @pl.when(n >= 1)
            def _():
                scatter_step(a, n - 1)
            if a == 0:
                @pl.when(n < NF)
                def _():
                    pass_step(1, n)
        loop(ND, body)
        if a == 0:
            for t in range(ND, NF):
                pass_step(1, t)
        scatter_step(a, ND - 1)

    down(0, wout, False)
    down(1, win, True)

    def last(n):
        for k in range(1, Z):
            dcopy(n, k).wait_recv()
        total = zf[0, gz, :, cols(n)]
        for k in range(1, Z):
            total = total + zrecv[k - 1, :, cols(n)].astype(f32)
        out_ref[:, cols(n)] = total
    loop(ND, last)

    for a in range(2):
        pltpu.make_async_copy(act.at[a], keeps[a], lsem.at[4 + a]).wait()
        for k in range(1, Z):
            zcopy(a, k).wait_send()
        for p in range(1, Y):
            for j in range(Z):
                ycopy(a, p, j).wait_send()

        def drain_f(t, a=a):
            for i in range(2):
                diagonal(a, t, i).wait_send()
                direct(a, t, i).wait_send()
                relay(a, t, i).wait_send()
                acopy(a, t, i).wait_send()
                apass(a, t, i).wait_send()
        loop(NF, drain_f)

        def drain_d(n, a=a):
            for p in range(1, Y):
                ccopy(a, n, p).wait_send()
            if a == 0:
                for k in range(1, Z):
                    dcopy(n, k).wait_send()
        loop(ND, drain_d)


def shards(sizes, tokens, grad_out, w_in, w_out):
    X, Y, Z = sizes["gx"], sizes["gy"], sizes["gz"]
    R, D = tokens.shape
    F = w_in.shape[1]
    T = R * Y * Z
    C, H = T // X, Z * R
    TN = math.gcd(math.gcd(F, D), 768)
    NF, ND = F // TN, D // TN
    f32, bf16 = jnp.float32, jnp.bfloat16
    dma = pltpu.SemaphoreType.DMA
    any_spec = pl.BlockSpec(memory_space=pl.ANY)
    vmem_spec = pl.BlockSpec(memory_space=pltpu.VMEM)
    assert X == 4
    *sends, out, gin, tok, grd, hid, slo = pl.pallas_call(
        functools.partial(fused_kernel, sizes),
        in_specs=[any_spec] * 4,
        out_specs=[vmem_spec] * (Z + 1) + [any_spec] * 4,
        out_shape=[jax.ShapeDtypeStruct((R, D), bf16)] * (Z - 1) + [
            jax.ShapeDtypeStruct((R, D), f32),
            jax.ShapeDtypeStruct((R, D), f32),
            jax.ShapeDtypeStruct((T, D), bf16),
            jax.ShapeDtypeStruct((T, D), bf16),
            jax.ShapeDtypeStruct((T, F), bf16),
            jax.ShapeDtypeStruct((T, F), bf16),
        ],
        scratch_shapes=[
            pltpu.VMEM((D, F), bf16),
            pltpu.VMEM((F, D), bf16),
            pltpu.VMEM((2, T, D), bf16),
            pltpu.VMEM((T, TN), f32),
            pltpu.VMEM((2, T, F), bf16),
            pltpu.VMEM((2, C, F), bf16),
            pltpu.VMEM((2, 2, C, F), bf16),
            pltpu.VMEM((2, C, F), f32),
            pltpu.VMEM((2, T, F), bf16),
            pltpu.VMEM((C, F), f32),
            pltpu.VMEM((2, T, D), bf16),
            pltpu.VMEM((2, H, D), f32),
            pltpu.VMEM((2, Y - 1, H, D), bf16),
            pltpu.VMEM((2, Z, R, D), f32),
            pltpu.VMEM((Z, R, D), bf16),
            pltpu.VMEM((Z - 1, R, D), bf16),
            dma((2,)),
            dma((6,)),
            dma((2, Z - 1)),
            dma((2, Z - 1)),
            dma((2, Y - 1, Z)),
            dma((2, Y - 1, Z)),
            dma((2, NF, 6)),
            dma((2, NF, 6)),
            dma((2, NF, 4)),
            dma((2, NF, 4)),
            dma((2, ND, Y - 1)),
            dma((2, ND, Y - 1)),
            dma((ND, Z - 1)),
            dma((ND, Z - 1)),
        ],
        compiler_params=pltpu.CompilerParams(
            collective_id=0, has_side_effects=True,
            vmem_limit_bytes=63 * 1024 * 1024,
        ),
    )(tokens, grad_out, w_in, w_out)
    moved = [
        lax.ppermute(sends[k - 1], "gz", [(z, (z + k) % Z) for z in range(Z)])
        for k in range(1, Z)
    ]
    g_in, g_out = weight_grads(tok, slo, hid, grd)
    for m in moved:
        gin = gin + m.astype(f32)
    return out, gin, g_in, g_out


def solution(mesh):
    rows = P(("gy", "gz"), "gx")
    w_in = P("gx", ("gy", "gz"))
    return jax.shard_map(
        functools.partial(shards, dict(mesh.shape)),
        mesh=mesh,
        in_specs=(rows, rows, w_in, rows),
        out_specs=(rows, rows, w_in, rows),
        check_vma=False,
    )
```
